1024 devices in a mesh: dp: 128 (over y_hi, z, core), section: 8 (over y_lo, x).
Axes of the slice: x: 4, y: 8 (y_hi: 4, y_lo: 2; y = y_hi * 2 + y_lo), z: 16, core: 2. Of those that a mesh axis runs over, the one named last changes fastest.
Arguments:
- layer_inputs: bfloat16 [8, 2, 256, 32, 4096], P('section', None, 'dp'), may hold values from -6 to 6
- saved_queries: bfloat16 [8, 2, 256, 32, 128], P('section', None, 'dp'), may hold values from -16 to 16
- saved_keys: bfloat16 [8, 2, 256, 32, 128], P('section', None, 'dp'), may hold values from -16 to 16
- held_weights: bfloat16 [8, 2, 2, 4096, 128], P('section'), may hold values from -0.15625 to 0.15625
- cotangent: bfloat16 [2, 256, 32, 4096], P(None, 'dp'), may hold values from -6 to 6
- valid_lengths: int32 [2, 256], P(None, 'dp'), may hold values from 2 to 32, as said below
Outputs:
- input_grads: bfloat16 [8, 2, 256, 32, 4096], P('section', None, 'dp')
- weight_grads: float32 [8, 2, 4096, 128], P('section', None, 'dp')
The draws below stay inside these ranges and needn't reach their ends.
Inputs may be any that keep to these rules, and one draw needn't show every extreme that they name: `valid_lengths`: some sequence has 32 valid tokens.
All inputs are finite; a program needn't handle non-finite values.
Results may differ from the reference program's by a relative error of at most 0.014.
Values may be sent and summed in bfloat16 or wider, within the bound.
A program may use at most 64 MiB of HBM per device.

```python
import math
import jax
import jax.numpy as jnp
from jax import lax

D = 4096
HEAD = 128
LEN = 32
BATCH = 256
N_SECTION = 8


def draw_pair(key):
    shape = (N_SECTION, 2, BATCH, LEN, HEAD)
    query_key, key_key = jax.random.split(jax.random.fold_in(key, 11), 2)
    queries = jax.random.normal(query_key, shape, jnp.float32)
    key_vectors = jax.random.normal(key_key, shape, jnp.float32)
    return (queries, key_vectors)


def draw_saved_queries(key, part):
    return draw_pair(key)[0].astype(jnp.bfloat16)


def draw_saved_keys(key, part):
    return draw_pair(key)[1].astype(jnp.bfloat16)


def draw_valid_lengths(key, part):
    drawn = jax.random.randint(jax.random.fold_in(key, 3), (2, BATCH), 2, LEN + 1)
    return drawn.at[0, 0].set(LEN).astype(jnp.int32)


def steps_of(rng, extent, cuts, least, high):
    def one(axis_at, blocks):
        heights = jax.random.uniform(jax.random.fold_in(jax.random.fold_in(rng, 6), axis_at), (blocks,), jnp.float32, least / len(cuts), high / len(cuts))
        return jnp.repeat(jnp.exp(heights), extent[axis_at] // blocks).reshape((-1,) + (1,) * (len(extent) - axis_at - 1))

    factor_of = one(*cuts[0])
    for cut in cuts[1:]:
        factor_of = factor_of * one(*cut)
    return factor_of


def centred(rng, extent, scale, bound, cuts=(), kind=jnp.bfloat16):
    factor_of = steps_of(rng, extent, cuts, -0.22, 0.18) if cuts else 1.0
    values = jax.random.normal(rng, extent, jnp.float32) * scale * factor_of
    return jnp.minimum(jnp.maximum(values, -bound), bound).astype(kind)


def setup_inputs(seed: int = 0) -> dict:
    streams_of = jax.random.split(jax.random.key(seed), 7)
    return {
        "layer_inputs": centred(streams_of[0], (N_SECTION, 2, BATCH, LEN, D), 1.0, 6.0, ((0, 8), (2, 128))),
        "saved_queries": draw_saved_queries(jax.random.fold_in(streams_of[6], 71), 0),
        "saved_keys": draw_saved_keys(jax.random.fold_in(streams_of[6], 71), 0),
        "held_weights": centred(streams_of[3], (N_SECTION, 2, 2, D, HEAD), (2 * (D * HEAD) ** 0.5) ** -0.5, 0.15625, ((0, 8),)),
        "cotangent": centred(streams_of[4], (2, BATCH, LEN, D), 1.0, 6.0, ((1, 128),)),
        "valid_lengths": draw_valid_lengths(jax.random.fold_in(streams_of[6], 71), 0),
    }


def attention_weights(queries, key_vectors, valid_lengths):
    length = queries.shape[-2]
    scores = jnp.einsum('...th,...sh->...ts', queries.astype(jnp.float32), key_vectors.astype(jnp.float32)) / math.sqrt(queries.shape[-1])
    row_pos = lax.broadcasted_iota(jnp.int32, (length, length), 0)
    col_pos = lax.broadcasted_iota(jnp.int32, (length, length), 1)
    allowed = (col_pos <= row_pos) & (col_pos < valid_lengths[..., None, None])
    scores = jnp.where(allowed, scores, -jnp.inf)
    row_max = lax.optimization_barrier(jnp.max(scores, axis=-1, keepdims=True))
    raised = jnp.where(allowed, jnp.exp(scores - row_max), 0.0)
    return (raised / lax.optimization_barrier(jnp.sum(raised, axis=-1, keepdims=True))).astype(jnp.bfloat16)

def head_backward(inputs, queries, key_vectors, lengths_now, value_w, output_w, upstream):
    attend = attention_weights(queries, key_vectors, lengths_now)
    seq_count, length, model_width = inputs.shape
    head_size = value_w.shape[1]
    flat_in = inputs.reshape(seq_count * length, model_width)
    flat_up = upstream.reshape(seq_count * length, model_width)
    values = jnp.dot(flat_in, value_w, preferred_element_type=jnp.float32).astype(jnp.bfloat16)
    values = values.reshape(seq_count, length, head_size)
    mixture = jnp.einsum('bts,bsh->bth', attend.astype(jnp.float32), values.astype(jnp.float32)).astype(jnp.bfloat16)
    out_grad = jnp.dot(flat_up, output_w, preferred_element_type=jnp.float32).astype(jnp.bfloat16)
    out_grad = out_grad.reshape(seq_count, length, head_size)
    val_grad = jnp.einsum('bts,bth->bsh', attend.astype(jnp.float32), out_grad.astype(jnp.float32)).astype(jnp.bfloat16)
    flat_vg = val_grad.reshape(seq_count * length, head_size)
    branch = jnp.dot(flat_vg, value_w.T, preferred_element_type=jnp.float32).reshape(seq_count, length, model_width)
    grad_input = (upstream.astype(jnp.float32) + branch).astype(jnp.bfloat16)
    grad_value = jnp.dot(flat_in.T, flat_vg, preferred_element_type=jnp.float32)
    grad_output = jnp.dot(flat_up.T, mixture.reshape(seq_count * length, head_size), preferred_element_type=jnp.float32)
    return (grad_input, grad_value, grad_output)

def reference(layer_inputs, saved_queries, saved_keys, held_weights, cotangent, valid_lengths):
    sections = layer_inputs.shape[0]
    grads_in = [[None] * sections, [None] * sections]
    value_terms = [[None] * sections, [None] * sections]
    output_terms = [[None] * sections, [None] * sections]
    for direction in range(2):
        upstream = cotangent[direction]
        visiting = range(sections - 1, -1, -1) if direction == 0 else range(sections)
        for section_no in visiting:
            grad_input, grad_value, grad_output = head_backward(layer_inputs[section_no, direction], saved_queries[section_no, direction], saved_keys[section_no, direction], valid_lengths[direction], held_weights[section_no, direction, 0], held_weights[section_no, direction, 1], upstream)
            grads_in[direction][section_no] = grad_input
            value_terms[direction][section_no] = grad_value
            output_terms[direction][section_no] = grad_output
            upstream = grad_input
    input_grads = jnp.stack([jnp.stack([grads_in[0][section_no], grads_in[1][section_no]]) for section_no in range(sections)])
    weight_grads = jnp.stack([jnp.stack([value_terms[0][section_no] + value_terms[1][sections - 1 - section_no], output_terms[0][section_no] + output_terms[1][sections - 1 - section_no]]) for section_no in range(sections)])
    return (input_grads, weight_grads)
```

```python
import math

import jax
import jax.numpy as jnp
from jax import lax
from jax.experimental import pallas as pl
from jax.experimental.pallas import tpu as pltpu
from jax.sharding import Mesh
from jax.sharding import PartitionSpec as P

SECTION = ("section_0", "section_1")
DP = ("dp_0", "dp_1", "dp_2")
MESH = pl.DeviceIdType.MESH
F32 = jnp.float32
BF16 = jnp.bfloat16
UNIT = 16


def transposed_attention(q, k, length_0, length_1):
    total = q.shape[0]
    half = total // 2
    scores = lax.dot_general(k, q, (((1,), (1,)), ((), ())), preferred_element_type=F32)
    scores = scores / math.sqrt(q.shape[1])
    key_pos = lax.broadcasted_iota(jnp.int32, (total, total), 0)
    query_pos = lax.broadcasted_iota(jnp.int32, (total, total), 1)
    limit = jnp.where(key_pos < half, length_0, length_1 + half)
    first = jnp.where(query_pos < half, 0, half)
    allowed = (key_pos <= query_pos) & (key_pos >= first) & (key_pos < limit)
    scores = jnp.where(allowed, scores, -1e30)
    top = jnp.max(scores, axis=0, keepdims=True)
    raised = jnp.where(allowed, jnp.exp(scores - top), 0.0)
    return (raised / jnp.sum(raised, axis=0, keepdims=True)).astype(BF16)


def make_kernel(n_y, n_z, n_x, sections, width, tokens, head):
    units = tokens // UNIT
    half_z = n_z // 2
    rows = width // (n_y * n_z)
    slab = width // n_y
    half_rows = rows // 2
    tile = min(1024, width)

    def kernel(
        lengths, q_ref, k_ref, x_hbm, w_hbm, cot_hbm, g_hbm, out_ref,
        wv, wo, acts, small, att, og, grads, part, ring_out, ring_in, y_out, y_in, z_sum,
        f_out, f_in, w_sem, x_sem, chain_send, chain_recv, g_sem, pair_send, pair_recv,
        rhs_send, rhs_recv, ring_send, ring_recv, y_send, y_recv, f_send, f_recv,
    ):
        y = lax.axis_index("dp_0")
        z = lax.axis_index("dp_1")
        core = lax.axis_index("dp_2")
        position = lax.axis_index("section_0") * n_x + lax.axis_index("section_1")
        other = 1 - core

        def at_position(j):
            return {"section_0": j // n_x, "section_1": j % n_x}

        partner = {"dp_2": other}
        z_next = {"dp_1": (z + 1) % n_z}
        z_prev = {"dp_1": (z + n_z - 1) % n_z}
        mirror = at_position(sections - 1 - position)
        mirror_other = {**mirror, "dp_2": other}
        y_peers = [{"dp_0": (y + d) % n_y} for d in range(1, n_y)]
        ahead = at_position((position + 1) % sections)
        behind = at_position((position + sections - 1) % sections)

        barrier = pltpu.get_barrier_semaphore()
        friends = [partner, z_next, z_prev, mirror, mirror_other, ahead, behind] + y_peers
        for friend in friends:
            pl.semaphore_signal(barrier, inc=1, device_id=friend, device_id_type=MESH)

        def row_of(m):
            half = units // 2
            return pl.multiple_of((1 - m // half) * UNIT + (m % half) * 2 * UNIT, UNIT)

        def cot_copy(r, m):
            at = pl.ds(row_of(m), UNIT)
            return pltpu.make_async_copy(
                cot_hbm.at[r, at], acts.at[0, r, at], chain_recv.at[r, m]
            )

        w_copies = []
        for r in range(2):
            w_copies.append(pltpu.make_async_copy(w_hbm.at[r, 1], wo.at[r], w_sem.at[r, 1]))
            w_copies.append(pltpu.make_async_copy(w_hbm.at[r, 0], wv.at[r], w_sem.at[r, 0]))
        x_copy = pltpu.make_async_copy(x_hbm, acts.at[1], x_sem)

        @pl.when(position == sections - 1)
        def _():
            for m in range(units):
                cot_copy(0, m).start()

        @pl.when(position == 0)
        def _():
            for m in range(units):
                cot_copy(1, m).start()

        for copy in w_copies:
            copy.start()
        x_copy.start()

        for r in range(2):
            att[r] = transposed_attention(q_ref[r], k_ref[r], lengths[r, 0], lengths[r, 1])
        og[...] = jnp.zeros_like(og)
        for copy in w_copies:
            copy.wait()
        x_copy.wait()
        pl.semaphore_wait(barrier, len(friends))

        def mixtures():
            for r in range(2):
                values = jnp.dot(acts[1, r], wv[r], preferred_element_type=F32).astype(BF16)
                small[0, r] = lax.dot_general(
                    att[r], values, (((0,), (0,)), ((), ())), preferred_element_type=F32
                ).astype(BF16)

        mid = (position != 0) & (position != sections - 1)

        @pl.when(mid)
        def _():
            mixtures()

        first = jnp.where(position < sections // 2, 1, 0)

        def goes_on(r):
            return jnp.where(r == 0, position > 0, position < sections - 1)

        def chain_copy(r, m):
            at = pl.ds(row_of(m), UNIT)
            return pltpu.make_async_remote_copy(
                src_ref=grads.at[r, at],
                dst_ref=acts.at[0, r, at],
                send_sem=chain_send.at[r, m],
                recv_sem=chain_recv.at[r, m],
                device_id=at_position(
                    jnp.clip(position + jnp.where(r == 0, -1, 1), 0, sections - 1)
                ),
                device_id_type=MESH,
            )

        def out_copy(r, m):
            at = pl.ds(row_of(m), UNIT)
            return pltpu.make_async_copy(grads.at[r, at], g_hbm.at[r, at], g_sem.at[r, m])

        def pair_copy(r, m):
            at = pl.ds(row_of(m), UNIT)
            return pltpu.make_async_remote_copy(
                src_ref=acts.at[core, r, at],
                dst_ref=acts.at[2, r, at],
                send_sem=pair_send.at[r, m],
                recv_sem=pair_recv.at[r, m],
                device_id=partner,
                device_id_type=MESH,
            )

        def rhs_copy(r):
            return pltpu.make_async_remote_copy(
                src_ref=small.at[core, r],
                dst_ref=small.at[2, r],
                send_sem=rhs_send.at[r],
                recv_sem=rhs_recv.at[r],
                device_id=partner,
                device_id_type=MESH,
            )

        def unit(r, m):
            at = pl.ds(row_of(m), UNIT)
            cot_copy(r, m).wait()
            pair_copy(r, m).start()
            og[r, at] = jnp.dot(acts[0, r, at], wo[r], preferred_element_type=F32).astype(BF16)
            val_grad = jnp.dot(att[r, at], og[r], preferred_element_type=F32).astype(BF16)
            small[1, r, at] = val_grad
            for t in range(width // tile):
                cols = pl.ds(t * tile, tile)
                branch = lax.dot_general(
                    val_grad, wv[r, cols], (((1,), (1,)), ((), ())), preferred_element_type=F32
                )
                grads[r, at, cols] = (acts[0, r, at, cols].astype(F32) + branch).astype(BF16)

            @pl.when(goes_on(r))
            def _():
                chain_copy(r, m).start()

            out_copy(r, m).start()

        @pl.loop(0, units)
        def _(m):
            unit(first, m)

        @pl.when(jnp.logical_not(mid))
        def _():
            mixtures()

        rhs_copy(first).start()

        @pl.loop(0, units)
        def _(m):
            unit(1 - first, m)

        rhs_copy(1 - first).start()

        def products(r):
            rhs_copy(r).wait_recv()

            @pl.loop(0, units)
            def _(m):
                pair_copy(r, m).wait_recv()

            for t in range(n_y):
                cols = pl.ds(t * slab, slab)
                product = lax.dot_general(
                    acts[other, r, :, cols], small[other, r],
                    (((0,), (0,)), ((), ())), preferred_element_type=F32,
                ) + lax.dot_general(
                    acts[2, r, :, cols], small[2, r],
                    (((0,), (0,)), ((), ())), preferred_element_type=F32,
                )
                part[r, t] = product.reshape(n_z, rows, head)

        products(first)
        products(1 - first)

        def ring_copy(way, r, s):
            return pltpu.make_async_remote_copy(
                src_ref=ring_out.at[way, r, s],
                dst_ref=ring_in.at[way, r, s],
                send_sem=ring_send.at[way, r, s],
                recv_sem=ring_recv.at[way, r, s],
                device_id=z_next if way == 0 else z_prev,
                device_id_type=MESH,
            )

        def ring_step(way, r, s, starts):
            shift = half_z - s if way == 0 else half_z + s
            target = lax.rem(z + shift, n_z)
            total = part[r, :, pl.ds(target, 1)].reshape(n_y, rows, head)
            if not starts:
                ring_copy(way, r, s - 1).wait_recv()
                total = total + ring_in[way, r, s - 1].astype(F32)
            ring_out[way, r, s] = total.astype(BF16)
            ring_copy(way, r, s).start()

        ring_step(0, 0, 0, True)
        ring_step(1, 1, 0, True)
        ring_step(1, 0, 1, True)
        ring_step(0, 1, 1, True)
        ring_step(0, 0, 1, False)
        ring_step(1, 1, 1, False)

        @pl.loop(2, half_z)
        def _(s):
            for way, r in ((1, 0), (0, 1), (0, 0), (1, 1)):
                ring_step(way, r, s, False)

        for r in range(2):
            total = part[r, :, pl.ds(z, 1)].reshape(n_y, rows, head)
            for way in range(2):
                ring_copy(way, r, half_z - 1).wait_recv()
                total = total + ring_in[way, r, half_z - 1].astype(F32)
            z_sum[:, r] = total

        def y_copy(d):
            return pltpu.make_async_remote_copy(
                src_ref=y_out.at[d - 1],
                dst_ref=y_in.at[d - 1],
                send_sem=y_send.at[d - 1],
                recv_sem=y_recv.at[d - 1],
                device_id=y_peers[d - 1],
                device_id_type=MESH,
            )

        for d in range(1, n_y):
            y_out[d - 1] = z_sum[lax.rem(y + d, n_y)].astype(BF16)
            y_copy(d).start()
        total = z_sum[y]
        for d in range(1, n_y):
            y_copy(d).wait_recv()
            total = total + y_in[d - 1].astype(F32)
        z_sum[y] = total

        def f_copy(slot):
            return pltpu.make_async_remote_copy(
                src_ref=f_out.at[slot],
                dst_ref=f_in.at[slot],
                send_sem=f_send.at[slot],
                recv_sem=f_recv.at[slot],
                device_id=(partner, mirror, mirror_other)[slot],
                device_id_type=MESH,
            )

        mine = pl.ds(pl.multiple_of(core * half_rows, half_rows), half_rows)
        theirs = pl.ds(pl.multiple_of(other * half_rows, half_rows), half_rows)
        f_out[1] = z_sum[y, 1, mine]
        f_copy(1).start()
        f_out[2] = z_sum[y, 1, theirs]
        f_copy(2).start()
        f_out[0] = z_sum[y, 0, theirs]
        f_copy(0).start()
        for slot in range(3):
            f_copy(slot).wait_recv()
        out_ref[core] = z_sum[y, 0, mine] + f_in[1]
        out_ref[other] = f_in[0] + f_in[2]

        for slot in range(3):
            f_copy(slot).wait_send()
        for d in range(1, n_y):
            y_copy(d).wait_send()
        for way, r in ((0, 0), (1, 1), (1, 0), (0, 1)):
            begin = 0 if way == r else 1

            @pl.loop(begin, half_z)
            def _(s):
                ring_copy(way, r, s).wait_send()

        for r in range(2):
            rhs_copy(r).wait_send()

            @pl.loop(0, units)
            def _(m):
                pair_copy(r, m).wait_send()
                out_copy(r, m).wait()

                @pl.when(goes_on(r))
                def _():
                    chain_copy(r, m).wait_send()

    dma = pltpu.SemaphoreType.DMA
    vmem = pltpu.VMEM
    scratch = [
        vmem((2, width, head), BF16),
        vmem((2, width, head), BF16),
        vmem((3, 2, tokens, width), BF16),
        vmem((3, 2, tokens, head), BF16),
        vmem((2, tokens, tokens), BF16),
        vmem((2, tokens, head), BF16),
        vmem((2, tokens, width), BF16),
        vmem((2, n_y, n_z, rows, head), F32),
        vmem((2, 2, half_z, n_y, rows, head), BF16),
        vmem((2, 2, half_z, n_y, rows, head), BF16),
        vmem((n_y - 1, 2, rows, head), BF16),
        vmem((n_y - 1, 2, rows, head), BF16),
        vmem((n_y, 2, rows, head), F32),
        vmem((3, half_rows, head), F32),
        vmem((3, half_rows, head), F32),
        dma((2, 2)),
        dma,
        dma((2, units)),
        dma((2, units)),
        dma((2, units)),
        dma((2, units)),
        dma((2, units)),
        dma((2,)),
        dma((2,)),
        dma((2, 2, half_z)),
        dma((2, 2, half_z)),
        dma((n_y - 1,)),
        dma((n_y - 1,)),
        dma((3,)),
        dma((3,)),
    ]
    any_space = pl.BlockSpec(memory_space=pl.ANY)
    in_vmem = pl.BlockSpec(memory_space=pltpu.VMEM)
    return pl.pallas_call(
        kernel,
        out_shape=(
            jax.ShapeDtypeStruct((2, tokens, width), BF16),
            jax.ShapeDtypeStruct((2, half_rows, head), F32),
        ),
        in_specs=[
            pl.BlockSpec(memory_space=pltpu.SMEM),
            in_vmem,
            in_vmem,
            any_space,
            any_space,
            any_space,
        ],
        out_specs=(any_space, in_vmem),
        scratch_shapes=scratch,
        compiler_params=pltpu.CompilerParams(
            collective_id=0, has_side_effects=True, vmem_limit_bytes=56 * 2**20
        ),
    )


def shards(layer_inputs, saved_queries, saved_keys, held_weights, cotangent, valid_lengths):
    _, _, seqs, length, width = layer_inputs.shape
    head = saved_queries.shape[-1]
    tokens = seqs * length
    call = make_kernel(
        lax.axis_size("dp_0"),
        lax.axis_size("dp_1"),
        lax.axis_size("section_1"),
        lax.axis_size(SECTION),
        width,
        tokens,
        head,
    )
    grads, weight_grads = call(
        valid_lengths,
        saved_queries.reshape(2, tokens, head),
        saved_keys.reshape(2, tokens, head),
        layer_inputs.reshape(2, tokens, width),
        held_weights[0],
        cotangent.reshape(2, tokens, width),
    )
    return (grads.reshape(1, 2, seqs, length, width), weight_grads[None])


def on_mesh(finer):
    in_specs = (
        P(SECTION, None, DP, None, None),
        P(SECTION, None, DP, None, None),
        P(SECTION, None, DP, None, None),
        P(SECTION, None, None, None, None),
        P(None, DP, None, None),
        P(None, DP),
    )
    out_specs = (P(SECTION, None, DP, None, None), P(SECTION, None, DP, None))
    return jax.shard_map(
        shards, mesh=finer, in_specs=in_specs, out_specs=out_specs, check_vma=False
    )


def solution(mesh):
    return on_mesh(
        Mesh(
            mesh.devices.reshape(4, 16, 2, 2, 4),
            ("dp_0", "dp_1", "dp_2", "section_0", "section_1"),
        )
    )
```
